32 devices in a mesh: mode: 16 (over z, x, core), rank: 2 (over y).
Axes of the slice: x: 2, y: 2, z: 4, core: 2. Of those that a mesh axis runs over, the one named last changes fastest.
Arguments:
- core_right: float32 [1024, 256, 1024], P('rank', 'mode'), may hold values from -0.1875 to 0.1875
- sketch_right: float32 [256, 256, 256], P('rank', 'mode'), may hold values from -0.0234375 to 0.0234375
- core_left: float32 [1024, 256, 1024], P('rank', 'mode'), may hold values from -0.1875 to 0.1875
- sketch_left: float32 [256, 256, 256], P('rank', 'mode'), may hold values from -0.0234375 to 0.0234375
- carry_in: float32 [1024, 256], P('rank'), may hold values from -6 to 6
Outputs:
- carry_out: float32 [1024, 256], P('rank')
The draws below stay inside these ranges and needn't reach their ends.
All inputs are finite; a program needn't handle non-finite values.
Results may differ from the reference program's by a relative error of at most 0.00013.
Values sent between devices are 32-bit elements; how exact they have to be, the bound alone decides.
No kernel may reach another device: no remote copies, remote signals or barrier semaphores. Data moves between devices by JAX's collectives and lax.ppermute only.
A program may use at most 128 MiB of HBM per device.

```python
import jax
import jax.numpy as jnp
from jax import lax

RANK = 1024
NM = 256
SK = 256


def level_of(key, shape, split, low, largest):
    loudness = 1.0
    for position, shards_of in split:
        draws = jax.random.uniform(jax.random.fold_in(jax.random.fold_in(key, 6), position), (shards_of,), jnp.float32, low / len(split), largest / len(split))
        loudness = loudness * jnp.repeat(jnp.exp(draws), shape[position] // shards_of).reshape((-1,) + (1,) * (len(shape) - 1 - position))
    return loudness


def scatter_about(key, dims, deviation, reach, split=(), held_as=jnp.bfloat16):
    drawn = deviation * jax.random.normal(key, dims, jnp.float32)
    if split:
        drawn = drawn * level_of(key, dims, split, -0.22, 0.18)
    return jnp.clip(drawn, -reach, reach).astype(held_as)


def setup_inputs(seed: int = 0) -> dict:
    seeds = jax.random.split(jax.random.key(seed), 6)
    core_right = scatter_about(seeds[0], (RANK, NM, RANK), RANK ** -0.5, 0.1875, ((0, 2), (1, 16)), jnp.float32)
    sketch_right = scatter_about(seeds[1], (SK, NM, SK), (NM * SK) ** -0.5, 0.0234375, ((0, 2), (1, 16)), jnp.float32)
    core_left = scatter_about(seeds[2], (RANK, NM, RANK), RANK ** -0.5, 0.1875, ((0, 2), (1, 16)), jnp.float32)
    sketch_left = scatter_about(seeds[3], (SK, NM, SK), (NM * SK) ** -0.5, 0.0234375, ((0, 2), (1, 16)), jnp.float32)
    carry_in = scatter_about(seeds[4], (RANK, SK), 1.0, 6.0, ((0, 2),), jnp.float32)
    return dict(core_right=core_right, sketch_right=sketch_right, core_left=core_left, sketch_left=sketch_left, carry_in=carry_in)


def chain_step(core, carried, sketch):
    hidden = jnp.einsum("aib,bc->aic", core, carried, precision=lax.Precision.HIGHEST)
    return jnp.einsum("aic,sic->as", hidden, sketch, precision=lax.Precision.HIGHEST)


def reference(core_right, sketch_right, core_left, sketch_left, carry_in):
    middle = chain_step(core_right, carry_in, sketch_right)
    return chain_step(core_left, middle, sketch_left)
```

```python
import functools

import jax
import jax.numpy as jnp
from jax import lax
from jax.experimental import pallas as pl
from jax.experimental.pallas import tpu as pltpu
from jax.sharding import PartitionSpec as P

F32, BF16 = jnp.float32, jnp.bfloat16
LANES = 128
HBM = pl.BlockSpec(memory_space=pl.ANY)
VMEM = pl.BlockSpec(memory_space=pltpu.VMEM)


def halves(x):
    high = x.astype(BF16)
    return high, (x - high.astype(F32)).astype(BF16)


def dot(a, b):
    return jnp.dot(a, b, preferred_element_type=F32)


def prepare_kernel(sketch_ref, out_ref):
    depth = sketch_ref.shape[2]
    for i in range(sketch_ref.shape[1]):
        high, low = halves(sketch_ref[:, i, :].T)
        out_ref[i, :depth] = high
        out_ref[i, depth:] = low


def hidden_loop(rows, slots, core_hbm, carried_ref, high, low, buf, sems, weights, tile):
    count, slices, depth = core_hbm.shape
    columns = carried_ref.shape[1]
    steps = count // rows

    def copy(k):
        slot = lax.rem(k, slots)
        return pltpu.make_async_copy(core_hbm.at[pl.ds(k * rows, rows)], buf.at[slot], sems.at[slot])

    for k in range(min(slots - 1, steps)):
        copy(k).start()
    h, l = halves(carried_ref[...])
    weights[0:depth] = h
    weights[depth : 2 * depth] = l
    weights[2 * depth :] = h

    def block(k, _):
        @pl.when(k + slots - 1 < steps)
        def _():
            copy(k + slots - 1).start()

        copy(k).wait()
        h, l = halves(buf[lax.rem(k, slots)].reshape(rows * slices, depth))
        result = dot(jnp.concatenate([h, h, l], axis=1), weights[...])
        for j in range(columns // LANES):
            tile[j] = result[:, j * LANES : (j + 1) * LANES]
        at = pl.ds(pl.multiple_of(k * rows, rows), rows)
        for i in range(slices):
            for j in range(columns // LANES):
                h, l = halves(tile[j, pl.ds(i, rows, stride=slices), :])
                high[i, at, j * LANES : (j + 1) * LANES] = h
                low[i, at, j * LANES : (j + 1) * LANES] = l
        return 0

    lax.fori_loop(0, steps, block, 0)


def multiply(group, first, high, low, sketches, out):
    slices = sketches[0].shape[0]
    depth = high.shape[2]
    group = min(group, slices)

    def body(g, _):
        xs, ys = [], [[] for _ in sketches]
        for t in range(group):
            i = g * group + t
            h = high[first + i]
            xs += [h, h, low[first + i]]
            for y, s in zip(ys, sketches):
                y += [s[i, :depth], s[i, depth:], s[i, :depth]]
        y = jnp.concatenate([jnp.concatenate(y, axis=0) for y in ys], axis=1)
        out[...] += dot(jnp.concatenate(xs, axis=1), y)
        return 0

    lax.fori_loop(0, slices // group, body, 0)


def product_kernel(group, firsts, high, low, *refs):
    base, chunks, out, prepared = refs[0], refs[1:-2], refs[-2], refs[-1]
    out[...] = jnp.zeros_like(out) if base is None else base[...]
    for first, chunk in zip(firsts, chunks):
        if prepared is not None:
            prepare_kernel(chunk, prepared)
            chunk = prepared
        multiply(group, first, high, low, [chunk], out)


def joined_kernel(group, cuts, high, low, *refs):
    out = refs[-1]
    out[...] = jnp.zeros_like(out)
    at = 0
    for first, width in cuts:
        multiply(group, first, high, low, refs[at : at + width], out)
        at += width


def hidden_shape(core, columns):
    return (core.shape[1], core.shape[0], columns)


def loop_scratch(core, columns, rows, slots):
    _, slices, depth = core.shape
    return [
        pltpu.VMEM((slots, rows, slices, depth), F32),
        pltpu.SemaphoreType.DMA((slots,)),
        pltpu.VMEM((3 * depth, columns), BF16),
        pltpu.VMEM((columns // LANES, rows * slices, LANES), F32),
    ]


def limit(mib):
    return pltpu.CompilerParams(vmem_limit_bytes=mib << 20)


ROWS, SLOTS, GROUP = 64, 3, 4


def hidden(core, carried):
    columns = carried.shape[1]
    out = jax.ShapeDtypeStruct(hidden_shape(core, columns), BF16)
    return pl.pallas_call(
        functools.partial(hidden_loop, ROWS, SLOTS),
        out_shape=(out, out),
        in_specs=[HBM, VMEM],
        out_specs=(VMEM, VMEM),
        scratch_shapes=loop_scratch(core, columns, ROWS, SLOTS),
        compiler_params=limit(32),
    )(core, carried)


def product(high, low, sketch, first=0, base=None):
    size, slices, depth = sketch.shape

    def kernel(high, low, *refs):
        product_kernel(GROUP, (first,), high, low, *(() if base is not None else (None,)), *refs)

    return pl.pallas_call(
        kernel,
        out_shape=jax.ShapeDtypeStruct((high.shape[1], size), F32),
        in_specs=[VMEM] * (3 + (base is not None)),
        out_specs=VMEM,
        scratch_shapes=[pltpu.VMEM((slices, 2 * depth, size), BF16)],
        compiler_params=limit(24),
    )(high, low, *(() if base is None else (base,)), sketch)


def joined(high, low, cuts, chunks):
    size = sum(s.shape[2] for s in chunks[: cuts[0][1]])
    return pl.pallas_call(
        functools.partial(joined_kernel, GROUP, cuts),
        out_shape=jax.ShapeDtypeStruct((high.shape[1], size), F32),
        in_specs=[VMEM] * (2 + len(chunks)),
        out_specs=VMEM,
        compiler_params=limit(24),
    )(high, low, *chunks)


def prepare(sketch):
    size, slices, depth = sketch.shape
    return pl.pallas_call(
        prepare_kernel,
        out_shape=jax.ShapeDtypeStruct((slices, 2 * depth, size), BF16),
        in_specs=[VMEM],
        out_specs=VMEM,
        compiler_params=limit(16),
    )(sketch)


def digit_groups(count):
    bits = count.bit_length() - 1
    groups, low = [], 0
    while low < bits:
        width = 1 if low < 2 else min(2, bits - low)
        groups.append((low, width))
        low += width
    return groups


def piece_of(index, groups):
    piece = 0
    for low, width in groups:
        piece = (piece << width) | ((index >> low) & ((1 << width) - 1))
    return piece


def partner(x, count, low, distance):
    return lax.ppermute(x, "mode", [(i, i ^ (distance << low)) for i in range(count)])


def shift(x, ranks, d):
    return lax.ppermute(x, "rank", [(i, (i + d) % ranks) for i in range(ranks)])


def reduce_scatter(x, count, groups):
    for low, width in groups:
        size = x.shape[0] >> width
        arrived = [partner(x[d * size : (d + 1) * size], count, low, d) for d in range(1, 1 << width)]
        x = sum(arrived, x[:size])
    return x


def all_gather(x, count, groups):
    for low, width in reversed(groups):
        x = jnp.concatenate([x] + [partner(x, count, low, d) for d in range(1, 1 << width)], axis=0)
    return x


def in_order(x, own):
    return jnp.take(x, own ^ jnp.arange(x.shape[0]), axis=0)


def by_rank(blocks, rank, axis):
    joined = jnp.concatenate(blocks[::-1], axis=axis)
    return jnp.roll(joined, (rank + 1) * blocks[0].shape[axis], axis=axis)


def quad_part(x, modes, mode):
    groups = digit_groups(modes)[:2]
    size = x.shape[0] >> len(groups)
    return lax.dynamic_slice_in_dim(x, piece_of(mode, groups) * size, size)


def all_rows(x, parts, modes, rank, mode):
    groups = digit_groups(modes)[:2]
    own = piece_of(mode, groups)
    blocks = [in_order(all_gather(part[None], modes, groups), own).reshape(x.shape) for part in parts]
    return by_rank([x] + blocks, rank, 0)


def shards(modes, ranks, core_right, sketch_right, core_left, sketch_left, carry_in):
    mode, rank = lax.axis_index("mode"), lax.axis_index("rank")
    groups = digit_groups(modes)
    own = piece_of(mode, groups)
    middle_slice = core_right.shape[1] // 2

    def pieces(x):
        return in_order(x.reshape((modes, x.shape[0] // modes) + x.shape[1:]), own)

    def cut(sketch):
        return sketch[:, :middle_slice], sketch[:, middle_slice:]

    def shifted(x):
        return [shift(x, ranks, d) for d in range(1, ranks)]

    (right_a, right_b), (left_a, left_b) = cut(sketch_right), cut(sketch_left)
    part = quad_part(carry_in, modes, mode)
    parts = shifted(part)
    parts, right_a, right_b = lax.optimization_barrier((parts, right_a, right_b))
    arrived_a, arrived_b = shifted(right_a), shifted(right_b)
    carried = all_rows(carry_in, parts, modes, rank, mode)
    high, low = hidden(core_right, carried)
    term = [product(high, low, sketch_right)]
    bases = [product(high, low, s) for s in arrived_a]
    arrived_b, left_a = lax.optimization_barrier((arrived_b, left_a))
    left_a_arrived = shifted(left_a)
    term += [product(high, low, s, middle_slice, base) for s, base in zip(arrived_b, bases)]
    middle = reduce_scatter(pieces(by_rank(term, rank, 1)), modes, groups)
    middle, left_a_arrived = lax.optimization_barrier((middle, left_a_arrived))
    middles, left_b = lax.optimization_barrier((shifted(middle), left_b))
    left_b_arrived = shifted(left_b)
    both = by_rank([middle] + middles, rank, 0)
    both = in_order(all_gather(both[None], modes, groups), own)
    carried = jnp.swapaxes(both, 0, 1).reshape(carried.shape)

    high, low = hidden(core_left, carried)
    own_a, own_b = cut(sketch_left)
    first, second = [own_a] + left_a_arrived, [own_b] + left_b_arrived
    if sketch_left.shape[0] % LANES:
        first, second = [jnp.concatenate(first)], [jnp.concatenate(second)]
    chunks = [prepare(s) for s in first + second]
    term = joined(high, low, ((0, len(first)), (middle_slice, len(second))), chunks)
    term = by_rank(jnp.split(term, ranks, axis=1), rank, 1)
    result = all_gather(reduce_scatter(pieces(term), modes, groups), modes, groups)
    return in_order(result, own).reshape(carry_in.shape)


def solution(mesh):
    modes, ranks = mesh.shape["mode"], mesh.shape["rank"]
    in_specs = (P("rank", "mode", None),) * 4 + (P("rank", None),)
    body = functools.partial(shards, modes, ranks)
    return jax.shard_map(body, mesh=mesh, in_specs=in_specs, out_specs=P("rank", None), check_vma=False)
```

```python
import functools

import jax
import jax.numpy as jnp
from jax import lax
from jax.experimental import pallas as pl
from jax.experimental.pallas import tpu as pltpu
from jax.sharding import PartitionSpec as P

F32, BF16 = jnp.float32, jnp.bfloat16
LANES = 128
HBM = pl.BlockSpec(memory_space=pl.ANY)
VMEM = pl.BlockSpec(memory_space=pltpu.VMEM)
SMEM = pl.BlockSpec(memory_space=pltpu.SMEM)


def halves(x):
    high = x.astype(BF16)
    return high, (x - high.astype(F32)).astype(BF16)


def dot(a, b):
    return jnp.dot(a, b, preferred_element_type=F32)


def prepare_kernel(sketch_ref, out_ref, axis=1):
    size = sketch_ref.shape[1 - axis]
    for i in range(sketch_ref.shape[axis]):
        high, low = halves((sketch_ref[:, i, :] if axis else sketch_ref[i]).T)
        out_ref[i, :, :size] = high
        out_ref[i, :, size:] = low


def hidden_loop(rows, slots, core_hbm, spread, high, low, buf, sems, weights, tile):
    count, slices, depth = core_hbm.shape
    columns = high.shape[2]
    steps = count // rows

    def copy(k):
        slot = lax.rem(k, slots)
        return pltpu.make_async_copy(core_hbm.at[pl.ds(k * rows, rows)], buf.at[slot], sems.at[slot])

    for k in range(min(slots - 1, steps)):
        copy(k).start()
    spread(weights)

    def block(k, _):
        @pl.when(k + slots - 1 < steps)
        def _():
            copy(k + slots - 1).start()

        copy(k).wait()
        h, l = halves(buf[lax.rem(k, slots)].reshape(rows * slices, depth))
        result = dot(jnp.concatenate([h, h, l], axis=1), weights[...])
        for j in range(columns // LANES):
            tile[j] = result[:, j * LANES : (j + 1) * LANES]
        at = pl.ds(pl.multiple_of(k * rows, rows), rows)
        for i in range(slices):
            for j in range(columns // LANES):
                h, l = halves(tile[j, pl.ds(i, rows, stride=slices), :])
                high[i, at, j * LANES : (j + 1) * LANES] = h
                low[i, at, j * LANES : (j + 1) * LANES] = l
        return 0

    lax.fori_loop(0, steps, block, 0)


def spread_whole(carried_ref, weights):
    depth = carried_ref.shape[0]
    h, l = halves(carried_ref[...])
    weights[0:depth] = h
    weights[depth : 2 * depth] = l
    weights[2 * depth :] = h


def first_kernel(rows, slots, core_hbm, carried_ref, sketch_ref, high, low, out, prepared, *scratch):
    hidden_loop(rows, slots, core_hbm, functools.partial(spread_whole, carried_ref), high, low, *scratch)
    prepare_kernel(sketch_ref, prepared)
    out[...] = jnp.zeros_like(out)
    multiply(0, sketch_ref.shape[1], high, low, [(prepared, 0)], out)


def hidden_kernel(rows, slots, core_hbm, carried_ref, high, low, *scratch):
    hidden_loop(rows, slots, core_hbm, functools.partial(spread_whole, carried_ref), high, low, *scratch)


def spread_pieces(ranks, place_ref, parts, weights):
    own, rank = place_ref[0], place_ref[1]
    _, _, rows, columns = parts[0].shape
    depth, width = weights.shape[0] // 3, columns // ranks
    position = 0
    for part in parts:
        for p in range(part.shape[0]):
            for d in range(ranks):
                source = lax.rem(rank - d + ranks, ranks)
                at = pl.multiple_of(source * (depth // ranks) + (own ^ position) * rows, rows)
                for e in range(ranks):
                    to = pl.ds(pl.multiple_of(lax.rem(source - e + ranks, ranks) * width, width), width)
                    h, l = halves(part[p, d, :, e * width : (e + 1) * width])
                    weights[pl.ds(at, rows), to] = h
                    weights[pl.ds(at + depth, rows), to] = l
                    weights[pl.ds(at + 2 * depth, rows), to] = h
            position += 1


def hidden_of_pieces_kernel(rows, slots, ranks, core_hbm, place_ref, *refs):
    parts, scratch = refs[:-6], refs[-6:]
    hidden_loop(rows, slots, core_hbm, functools.partial(spread_pieces, ranks, place_ref, parts), *scratch)


def multiply(first, count, high, low, sketches, out):
    def add(start, size):
        slices = range(size)
        h = jnp.concatenate([high[first + start + t] for t in slices], axis=1)
        l = jnp.concatenate([low[first + start + t] for t in slices], axis=1)
        sums, highs = [], []
        for s, at in sketches:
            both = jnp.concatenate([s[at + start + t] for t in slices], axis=0)
            width = both.shape[1] // 2
            result = dot(h, both)
            sums.append(result[:, :width] + result[:, width:])
            highs.append(both[:, :width])
        out[...] += jnp.concatenate(sums, axis=1) + dot(l, jnp.concatenate(highs, axis=1))

    def body(g, _):
        add(g * GROUP, GROUP)
        return 0

    whole = count // GROUP
    lax.fori_loop(0, whole, body, 0)
    if count % GROUP:
        add(whole * GROUP, count % GROUP)


def store(place_ref, acc, out):
    if len(out.shape) == 2:
        out[...] = acc[...]
        return
    count, rows, _ = out.shape
    for p in range(count):
        out[p] = acc[pl.ds(pl.multiple_of((place_ref[0] ^ p) * rows, rows), rows), :]


def second_kernel(place_ref, high, low, own_ref, *refs):
    sketches, (out, prepared, acc) = refs[:-3], refs[-3:]
    width = own_ref.shape[1]
    acc[:, :width] = own_ref[...]
    for d, sketch in enumerate(sketches):
        at = slice((d + 1) * width, (d + 2) * width)
        acc[:, at] = jnp.zeros_like(own_ref)
        prepare_kernel(sketch, prepared)
        multiply(0, sketch.shape[1], high, low, [(prepared, 0)], acc.at[:, at])
    store(place_ref, acc, out)


def joined_kernel(early, place_ref, high, low, *refs):
    sketches, (out, acc) = refs[:-2], refs[-2:]
    acc[...] = jnp.zeros_like(acc)
    slices = high.shape[0]
    firsts, rests, at = [], [], 0
    while at < len(sketches):
        if sketches[at].shape[0] == slices:
            firsts.append((sketches[at], 0))
            rests.append((sketches[at], early))
            at += 1
        else:
            firsts.append((sketches[at], 0))
            rests.append((sketches[at + 1], 0))
            at += 2
    multiply(0, early, high, low, firsts, acc)
    multiply(early, slices - early, high, low, rests, acc)
    store(place_ref, acc, out)


def settle_kernel(ranks, place_ref, *refs):
    parts, out = refs[:-1], refs[-1]
    _, rows, columns = parts[0].shape
    width = columns // ranks
    position = 0
    for part in parts:
        for p in range(part.shape[0]):
            at = pl.ds(pl.multiple_of((place_ref[0] ^ position) * rows, rows), rows)
            for e in range(ranks):
                to = lax.rem(place_ref[1] - e + ranks, ranks) * width
                out[at, pl.ds(pl.multiple_of(to, width), width)] = part[p, :, e * width : (e + 1) * width]
            position += 1


def hidden_shape(core, columns):
    return (core.shape[1], core.shape[0], columns)


def loop_scratch(core, columns, rows, slots):
    _, slices, depth = core.shape
    return [
        pltpu.VMEM((slots, rows, slices, depth), F32),
        pltpu.SemaphoreType.DMA((slots,)),
        pltpu.VMEM((3 * depth, columns), BF16),
        pltpu.VMEM((columns // LANES, rows * slices, LANES), F32),
    ]


def limit(mib):
    return pltpu.CompilerParams(vmem_limit_bytes=mib << 20)


ROWS, SLOTS, GROUP = 64, 3, 4


def cost(flops, size):
    return pl.CostEstimate(flops=flops, bytes_accessed=size, transcendentals=0)


def hidden(core, carried, place=None):
    count, slices, depth = core.shape
    columns = (carried if place is None else carried[0]).shape[-1]
    out = jax.ShapeDtypeStruct(hidden_shape(core, columns), BF16)
    if place is None:
        kernel, operands = functools.partial(hidden_kernel, ROWS, SLOTS), (carried,)
    else:
        ranks = carried[0].shape[1]
        kernel, operands = functools.partial(hidden_of_pieces_kernel, ROWS, SLOTS, ranks), (place, *carried)
    return pl.pallas_call(
        kernel,
        out_shape=(out, out),
        in_specs=[HBM] + ([VMEM] if place is None else [SMEM] + [VMEM] * len(carried)),
        out_specs=(VMEM, VMEM),
        scratch_shapes=loop_scratch(core, columns, ROWS, SLOTS),
        compiler_params=limit(32),
        cost_estimate=cost(6 * count * slices * depth * columns, 4 * core.size) if place is None else cost(1, 1),
    )(core, *operands)


def product_cost(high, slices, columns):
    return cost(6 * high.shape[1] * slices * high.shape[2] * columns, 4 * high.size)


def first_step(core, carried, sketch):
    size, slices, depth = sketch.shape
    columns = carried.shape[1]
    out = jax.ShapeDtypeStruct(hidden_shape(core, columns), BF16)
    return pl.pallas_call(
        functools.partial(first_kernel, ROWS, SLOTS),
        out_shape=(out, out, jax.ShapeDtypeStruct((core.shape[0], size), F32)),
        in_specs=[HBM, VMEM, VMEM],
        out_specs=(VMEM,) * 3,
        scratch_shapes=[pltpu.VMEM((slices, depth, 2 * size), BF16)] + loop_scratch(core, columns, ROWS, SLOTS),
        compiler_params=limit(36),
        cost_estimate=cost(6 * core.size * columns, 4 * core.size),
    )(core, carried, sketch)


def out_shape(rows, columns, count):
    return jax.ShapeDtypeStruct((count, rows // count, columns) if count else (rows, columns), F32)


def second_product(place, high, low, own, sketches, count):
    size, slices, depth = sketches[0].shape
    rows, columns = high.shape[1], size * (1 + len(sketches))
    return pl.pallas_call(
        second_kernel,
        out_shape=out_shape(rows, columns, count),
        in_specs=[SMEM] + [VMEM] * (3 + len(sketches)),
        out_specs=VMEM,
        scratch_shapes=[pltpu.VMEM((slices, depth, 2 * size), BF16), pltpu.VMEM((rows, columns), F32)],
        compiler_params=limit(24),
        cost_estimate=product_cost(high, slices, columns - size),
    )(place, high, low, own, *sketches)


def joined(place, high, low, early, chunks, columns, count):
    rows = high.shape[1]
    return pl.pallas_call(
        functools.partial(joined_kernel, early),
        out_shape=out_shape(rows, columns, count),
        in_specs=[SMEM] + [VMEM] * (2 + len(chunks)),
        out_specs=VMEM,
        scratch_shapes=[pltpu.VMEM((rows, columns), F32)],
        compiler_params=limit(24),
        cost_estimate=product_cost(high, high.shape[0], columns),
    )(place, high, low, *chunks)


def settle(place, parts, ranks):
    _, rows, columns = parts[0].shape
    return pl.pallas_call(
        functools.partial(settle_kernel, ranks),
        out_shape=jax.ShapeDtypeStruct((rows * sum(p.shape[0] for p in parts), columns), F32),
        in_specs=[SMEM] + [VMEM] * len(parts),
        out_specs=VMEM,
        compiler_params=limit(8),
    )(place, *parts)


def prepare(sketch, axis=1):
    slices, size, depth = sketch.shape[axis], sketch.shape[1 - axis], sketch.shape[2]
    return pl.pallas_call(
        functools.partial(prepare_kernel, axis=axis),
        out_shape=jax.ShapeDtypeStruct((slices, depth, 2 * size), BF16),
        in_specs=[VMEM],
        out_specs=VMEM,
        compiler_params=limit(16),
        cost_estimate=cost(0, 8 * sketch.size),
    )(sketch)


def digit_groups(count):
    bits = count.bit_length() - 1
    groups, low = [], 0
    while low < bits:
        width = 1 if low < 2 else min(2, bits - low)
        groups.append((low, width))
        low += width
    return groups


def piece_of(index, groups):
    piece = 0
    for low, width in groups:
        piece = (piece << width) | ((index >> low) & ((1 << width) - 1))
    return piece


def partner(x, count, low, distance):
    return lax.ppermute(x, "mode", [(i, i ^ (distance << low)) for i in range(count)])


def shift(x, ranks, d):
    return lax.ppermute(x, "rank", [(i, (i + d) % ranks) for i in range(ranks)])


def reduce_scatter(x, count, groups):
    for low, width in groups:
        size = x.shape[0] >> width
        arrived = [partner(x[d * size : (d + 1) * size], count, low, d) for d in range(1, 1 << width)]
        x = sum(arrived, x[:size])
    return x


def all_gather_parts(x, count, groups):
    parts = [x]
    for low, width in reversed(groups):
        x = jnp.concatenate(parts, axis=0)
        parts = [x] + [partner(x, count, low, d) for d in range(1, 1 << width)]
    return parts


def all_gather(x, count, groups):
    return jnp.concatenate(all_gather_parts(x, count, groups), axis=0)


def in_order(x, own):
    return jnp.take(x, own ^ jnp.arange(x.shape[0]), axis=0)


def by_rank(blocks, rank, axis):
    joined = jnp.concatenate(blocks[::-1], axis=axis)
    return jnp.roll(joined, (rank + 1) * blocks[0].shape[axis], axis=axis)


def quad_part(x, modes, mode):
    groups = digit_groups(modes)[:2]
    size = x.shape[0] >> len(groups)
    return lax.dynamic_slice_in_dim(x, piece_of(mode, groups) * size, size)


def all_rows(x, parts, modes, rank, mode):
    groups = digit_groups(modes)[:2]
    own = piece_of(mode, groups)
    blocks = [in_order(all_gather(part[None], modes, groups), own).reshape(x.shape) for part in parts]
    return by_rank([x] + blocks, rank, 0)


def shards(modes, ranks, core_right, sketch_right, core_left, sketch_left, carry_in):
    mode, rank = lax.axis_index("mode"), lax.axis_index("rank")
    groups = digit_groups(modes)
    own = piece_of(mode, groups)
    place = jnp.stack([own, rank])
    slices, size = core_right.shape[1], sketch_right.shape[0]
    early = max(1, slices // 8)
    count = modes if carry_in.shape[0] % (16 * modes) == 0 and size % LANES == 0 else 0

    def shifted(x):
        return [shift(x, ranks, d) for d in range(1, ranks)]

    def scattered(term):
        if not count:
            term = by_rank(jnp.split(term, ranks, axis=1), rank, 1)
            term = in_order(term.reshape((modes, term.shape[0] // modes) + term.shape[1:]), own)
        return reduce_scatter(term, modes, groups)

    sketch_slices = jnp.swapaxes(sketch_left, 0, 1)
    left_a, left_b = sketch_slices[:early], sketch_slices[early:]
    part = quad_part(carry_in, modes, mode)
    parts = shifted(part)
    _, right = lax.optimization_barrier((part, sketch_right))
    arrived = shifted(right)
    carried = all_rows(carry_in, parts, modes, rank, mode)
    high, low, term = first_step(core_right, carried, sketch_right)
    arrived, left_a = lax.optimization_barrier((arrived, left_a))
    left_a_arrived = shifted(left_a)
    term = second_product(place, high, low, term, arrived, count)
    middle = scattered(term)
    middle, left_a_arrived = lax.optimization_barrier((middle, left_a_arrived))
    middles, left_b = lax.optimization_barrier((shifted(middle), left_b))
    left_b_arrived = shifted(left_b)
    if count:
        both = jnp.concatenate([middle] + middles)[None]
        high, low = hidden(core_left, all_gather_parts(both, modes, groups), place)
    else:
        both = by_rank([middle] + middles, rank, 0)[None]
        both = in_order(all_gather(both, modes, groups), own)
        high, low = hidden(core_left, jnp.swapaxes(both, 0, 1).reshape(carried.shape))

    if count:
        chunks = [prepare(sketch_left)]
        for pair in zip(left_a_arrived, left_b_arrived):
            chunks += [prepare(x, 0) for x in pair]
    else:
        whole = [jnp.concatenate(pair) for pair in zip(left_a_arrived, left_b_arrived)]
        chunks = [prepare(jnp.concatenate([sketch_slices] + whole, axis=1), 0)]
    term = joined(place, high, low, early, chunks, size * ranks, count)
    result = all_gather_parts(scattered(term), modes, groups)
    if count:
        return settle(place, result, ranks)
    return in_order(jnp.concatenate(result, axis=0), own).reshape(carry_in.shape)


def solution(mesh):
    modes, ranks = mesh.shape["mode"], mesh.shape["rank"]
    in_specs = (P("rank", "mode", None),) * 4 + (P("rank", None),)
    body = functools.partial(shards, modes, ranks)
    return jax.shard_map(body, mesh=mesh, in_specs=in_specs, out_specs=P("rank", None), check_vma=False)
```

```python
import functools

import jax
import jax.numpy as jnp
from jax import lax
from jax.experimental import pallas as pl
from jax.experimental.pallas import tpu as pltpu
from jax.sharding import PartitionSpec as P

F32, BF16 = jnp.float32, jnp.bfloat16
LANES = 128
HBM = pl.BlockSpec(memory_space=pl.ANY)
VMEM = pl.BlockSpec(memory_space=pltpu.VMEM)
SMEM = pl.BlockSpec(memory_space=pltpu.SMEM)


def halves(x):
    high = x.astype(BF16)
    return high, (x - high.astype(F32)).astype(BF16)


def dot(a, b):
    return jnp.dot(a, b, preferred_element_type=F32)


def prepare_kernel(sketch_ref, out_ref, axis=1):
    size = sketch_ref.shape[1 - axis]
    for i in range(sketch_ref.shape[axis]):
        high, low = halves((sketch_ref[:, i, :] if axis else sketch_ref[i]).T)
        out_ref[i, :, :size] = high
        out_ref[i, :, size:] = low


def hidden_loop(core_hbm, spread, high, low, buf, sems, weights):
    rows, slices, _ = core_hbm.shape
    slots, width = buf.shape[0], buf.shape[1] // rows
    steps = slices // width

    def copies(k):
        slot = lax.rem(k, slots)
        return [
            pltpu.make_async_copy(core_hbm.at[:, k * width + u, :], buf.at[slot, pl.ds(u * rows, rows)], sems.at[slot, u])
            for u in range(width)
        ]

    for k in range(min(slots - 1, steps)):
        for copy in copies(k):
            copy.start()
    spread(weights)

    def block(k, _):
        @pl.when(k + slots - 1 < steps)
        def _():
            for copy in copies(k + slots - 1):
                copy.start()

        for copy in copies(k):
            copy.wait()
        h, l = halves(buf[lax.rem(k, slots)])
        h, l = halves(dot(jnp.concatenate([h, h, l], axis=1), weights[...]))
        for u in range(width):
            high[k * width + u] = h[u * rows : (u + 1) * rows]
            low[k * width + u] = l[u * rows : (u + 1) * rows]
        return 0

    lax.fori_loop(0, steps, block, 0)


def spread_whole(carried_ref, weights):
    depth = carried_ref.shape[0]
    h, l = halves(carried_ref[...])
    weights[0:depth] = h
    weights[depth : 2 * depth] = l
    weights[2 * depth :] = h


def first_kernel(core_hbm, carried_ref, sketch_ref, high, low, out, prepared, *scratch):
    hidden_loop(core_hbm, functools.partial(spread_whole, carried_ref), high, low, *scratch)
    prepare_kernel(sketch_ref, prepared)
    out[...] = jnp.zeros_like(out)
    multiply(high, low, [[prepared]], out)


def hidden_kernel(core_hbm, carried_ref, high, low, *scratch):
    hidden_loop(core_hbm, functools.partial(spread_whole, carried_ref), high, low, *scratch)


def spread_pieces(ranks, place_ref, parts, weights):
    own, rank = place_ref[0], place_ref[1]
    _, _, rows, columns = parts[0].shape
    depth, width = weights.shape[0] // 3, columns // ranks
    position = 0
    for part in parts:
        for p in range(part.shape[0]):
            for d in range(ranks):
                source = lax.rem(rank - d + ranks, ranks)
                at = pl.multiple_of(source * (depth // ranks) + (own ^ position) * rows, rows)
                for e in range(ranks):
                    to = pl.ds(pl.multiple_of(lax.rem(source - e + ranks, ranks) * width, width), width)
                    h, l = halves(part[p, d, :, e * width : (e + 1) * width])
                    weights[pl.ds(at, rows), to] = h
                    weights[pl.ds(at + depth, rows), to] = l
                    weights[pl.ds(at + 2 * depth, rows), to] = h
            position += 1


def hidden_of_pieces_kernel(ranks, core_hbm, place_ref, *refs):
    parts, scratch = refs[:-5], refs[-5:]
    hidden_loop(core_hbm, functools.partial(spread_pieces, ranks, place_ref, parts), *scratch)


def multiply(high, low, sketches, out):
    where = [[(ref, i) for ref in refs for i in range(ref.shape[0])] for refs in sketches]
    for start in range(0, high.shape[0], GROUP):
        slices = range(start, min(start + GROUP, high.shape[0]))
        h = jnp.concatenate([high[i] for i in slices], axis=1)
        l = jnp.concatenate([low[i] for i in slices], axis=1)
        sums, highs = [], []
        for places in where:
            both = jnp.concatenate([places[i][0][places[i][1]] for i in slices], axis=0)
            width = both.shape[1] // 2
            result = dot(h, both)
            sums.append(result[:, :width] + result[:, width:])
            highs.append(both[:, :width])
        out[...] += jnp.concatenate(sums, axis=1) + dot(l, jnp.concatenate(highs, axis=1))


def store(place_ref, acc, out):
    if len(out.shape) == 2:
        out[...] = acc[...]
        return
    count, rows, _ = out.shape
    for p in range(count):
        out[p] = acc[pl.ds(pl.multiple_of((place_ref[0] ^ p) * rows, rows), rows), :]


def second_kernel(place_ref, high, low, own_ref, *refs):
    sketches, (out, prepared, acc) = refs[:-3], refs[-3:]
    width = own_ref.shape[1]
    acc[:, :width] = own_ref[...]
    for d, sketch in enumerate(sketches):
        at = slice((d + 1) * width, (d + 2) * width)
        acc[:, at] = jnp.zeros_like(own_ref)
        prepare_kernel(sketch, prepared)
        multiply(high, low, [[prepared]], acc.at[:, at])
    store(place_ref, acc, out)


def joined_kernel(counts, place_ref, high, low, *refs):
    chunks, (out, acc) = list(refs[:-2]), refs[-2:]
    acc[...] = jnp.zeros_like(acc)
    multiply(high, low, [[chunks.pop(0) for _ in range(count)] for count in counts], acc)
    store(place_ref, acc, out)


def settle_kernel(ranks, place_ref, *refs):
    parts, out = refs[:-1], refs[-1]
    _, rows, columns = parts[0].shape
    width = columns // ranks
    position = 0
    for part in parts:
        for p in range(part.shape[0]):
            at = pl.ds(pl.multiple_of((place_ref[0] ^ position) * rows, rows), rows)
            for e in range(ranks):
                to = lax.rem(place_ref[1] - e + ranks, ranks) * width
                out[at, pl.ds(pl.multiple_of(to, width), width)] = part[p, :, e * width : (e + 1) * width]
            position += 1


def hidden_shape(core, columns):
    return (core.shape[1], core.shape[0], columns)


def loop_scratch(core, columns):
    rows, slices, depth = core.shape
    width = 2 - slices % 2
    return [
        pltpu.VMEM((SLOTS, width * rows, depth), F32),
        pltpu.SemaphoreType.DMA((SLOTS, width)),
        pltpu.VMEM((3 * depth, columns), BF16),
    ]


def limit(mib):
    return pltpu.CompilerParams(vmem_limit_bytes=mib << 20)


SLOTS, GROUP = 3, 8


def cost(flops, size):
    return pl.CostEstimate(flops=flops, bytes_accessed=size, transcendentals=0)


def hidden(core, carried, place=None):
    count, slices, depth = core.shape
    columns = (carried if place is None else carried[0]).shape[-1]
    out = jax.ShapeDtypeStruct(hidden_shape(core, columns), BF16)
    if place is None:
        kernel, operands = hidden_kernel, (carried,)
    else:
        ranks = carried[0].shape[1]
        kernel, operands = functools.partial(hidden_of_pieces_kernel, ranks), (place, *carried)
    return pl.pallas_call(
        kernel,
        out_shape=(out, out),
        in_specs=[HBM] + ([VMEM] if place is None else [SMEM] + [VMEM] * len(carried)),
        out_specs=(VMEM, VMEM),
        scratch_shapes=loop_scratch(core, columns),
        compiler_params=limit(32),
        cost_estimate=cost(6 * count * slices * depth * columns, 4 * core.size) if place is None else cost(1, 1),
    )(core, *operands)


def product_cost(high, slices, columns):
    return cost(6 * high.shape[1] * slices * high.shape[2] * columns, 4 * high.size)


def first_step(core, carried, sketch):
    size, slices, depth = sketch.shape
    columns = carried.shape[1]
    out = jax.ShapeDtypeStruct(hidden_shape(core, columns), BF16)
    return pl.pallas_call(
        first_kernel,
        out_shape=(out, out, jax.ShapeDtypeStruct((core.shape[0], size), F32)),
        in_specs=[HBM, VMEM, VMEM],
        out_specs=(VMEM,) * 3,
        scratch_shapes=[pltpu.VMEM((slices, depth, 2 * size), BF16)] + loop_scratch(core, columns),
        compiler_params=limit(36),
        cost_estimate=cost(6 * core.size * columns, 4 * core.size),
    )(core, carried, sketch)


def out_shape(rows, columns, count):
    return jax.ShapeDtypeStruct((count, rows // count, columns) if count else (rows, columns), F32)


def second_product(place, high, low, own, sketches, count):
    size, slices, depth = sketches[0].shape
    rows, columns = high.shape[1], size * (1 + len(sketches))
    return pl.pallas_call(
        second_kernel,
        out_shape=out_shape(rows, columns, count),
        in_specs=[SMEM] + [VMEM] * (3 + len(sketches)),
        out_specs=VMEM,
        scratch_shapes=[pltpu.VMEM((slices, depth, 2 * size), BF16), pltpu.VMEM((rows, columns), F32)],
        compiler_params=limit(24),
        cost_estimate=product_cost(high, slices, columns - size),
    )(place, high, low, own, *sketches)


def joined(place, high, low, counts, chunks, columns, count):
    rows = high.shape[1]
    return pl.pallas_call(
        functools.partial(joined_kernel, counts),
        out_shape=out_shape(rows, columns, count),
        in_specs=[SMEM] + [VMEM] * (2 + len(chunks)),
        out_specs=VMEM,
        scratch_shapes=[pltpu.VMEM((rows, columns), F32)],
        compiler_params=limit(24),
        cost_estimate=product_cost(high, high.shape[0], columns),
    )(place, high, low, *chunks)


def settle(place, parts, ranks):
    _, rows, columns = parts[0].shape
    return pl.pallas_call(
        functools.partial(settle_kernel, ranks),
        out_shape=jax.ShapeDtypeStruct((rows * sum(p.shape[0] for p in parts), columns), F32),
        in_specs=[SMEM] + [VMEM] * len(parts),
        out_specs=VMEM,
        compiler_params=limit(8),
    )(place, *parts)


def prepare(sketch, axis=1):
    slices, size, depth = sketch.shape[axis], sketch.shape[1 - axis], sketch.shape[2]
    return pl.pallas_call(
        functools.partial(prepare_kernel, axis=axis),
        out_shape=jax.ShapeDtypeStruct((slices, depth, 2 * size), BF16),
        in_specs=[VMEM],
        out_specs=VMEM,
        compiler_params=limit(16),
        cost_estimate=cost(0, 8 * sketch.size),
    )(sketch)


def digit_groups(count):
    bits = count.bit_length() - 1
    groups, low = [], 0
    while low < bits:
        width = 1 if low < 2 else min(2, bits - low)
        groups.append((low, width))
        low += width
    return groups


def far_first(digit, width):
    return digit ^ ((digit & 1) << 1) if width == 2 else digit


def piece_of(index, groups):
    piece = 0
    for low, width in groups:
        piece = (piece << width) | far_first((index >> low) & ((1 << width) - 1), width)
    return piece


def partner(x, count, low, width, position):
    distance = far_first(position, width) << low
    return lax.ppermute(x, "mode", [(i, i ^ distance) for i in range(count)])


def shift(x, ranks, d):
    return lax.ppermute(x, "rank", [(i, (i + d) % ranks) for i in range(ranks)])


def reduce_scatter(x, count, groups):
    for low, width in groups:
        size = x.shape[0] >> width
        arrived = [partner(x[d * size : (d + 1) * size], count, low, width, d) for d in range(1, 1 << width)]
        x = sum(arrived, x[:size])
    return x


def all_gather_parts(x, count, groups):
    parts = [x]
    for low, width in reversed(groups):
        x = jnp.concatenate(parts, axis=0)
        parts = [x] + [partner(x, count, low, width, d) for d in range(1, 1 << width)]
    return parts


def all_gather(x, count, groups):
    return jnp.concatenate(all_gather_parts(x, count, groups), axis=0)


def in_order(x, own):
    return jnp.take(x, own ^ jnp.arange(x.shape[0]), axis=0)


def by_rank(blocks, rank, axis):
    joined = jnp.concatenate(blocks[::-1], axis=axis)
    return jnp.roll(joined, (rank + 1) * blocks[0].shape[axis], axis=axis)


def quad_part(x, modes, mode):
    groups = digit_groups(modes)[:2]
    size = x.shape[0] >> len(groups)
    return lax.dynamic_slice_in_dim(x, piece_of(mode, groups) * size, size)


def all_rows(x, parts, modes, rank, mode):
    groups = digit_groups(modes)[:2]
    own = piece_of(mode, groups)
    blocks = [in_order(all_gather(part[None], modes, groups), own).reshape(x.shape) for part in parts]
    return by_rank([x] + blocks, rank, 0)


def shards(modes, ranks, core_right, sketch_right, core_left, sketch_left, carry_in):
    mode, rank = lax.axis_index("mode"), lax.axis_index("rank")
    groups = digit_groups(modes)
    own = piece_of(mode, groups)
    place = jnp.stack([own, rank])
    slices, size = core_right.shape[1], sketch_right.shape[0]
    early = max(1, slices // 4)
    count = modes if carry_in.shape[0] % (16 * modes) == 0 and size % LANES == 0 else 0

    def shifted(x):
        return [shift(x, ranks, d) for d in range(1, ranks)]

    def scattered(term):
        if not count:
            term = by_rank(jnp.split(term, ranks, axis=1), rank, 1)
            term = in_order(term.reshape((modes, term.shape[0] // modes) + term.shape[1:]), own)
        return reduce_scatter(term, modes, groups)

    sketch_slices = jnp.swapaxes(sketch_left, 0, 1)
    left_a, left_b = sketch_slices[:early], sketch_slices[early:]
    part = quad_part(carry_in, modes, mode)
    parts = shifted(part)
    _, right = lax.optimization_barrier((part, sketch_right))
    arrived = shifted(right)
    carried = all_rows(carry_in, parts, modes, rank, mode)
    high, low, term = first_step(core_right, carried, sketch_right)
    arrived, left_a = lax.optimization_barrier((arrived, left_a))
    left_a_arrived = shifted(left_a)
    term = second_product(place, high, low, term, arrived, count)
    middle = scattered(term)
    middle, left_a_arrived = lax.optimization_barrier((middle, left_a_arrived))
    middles, left_b = lax.optimization_barrier((shifted(middle), left_b))
    left_b_arrived = shifted(left_b)
    if count:
        both = jnp.concatenate([middle] + middles)[None]
        high, low = hidden(core_left, all_gather_parts(both, modes, groups), place)
    else:
        both = by_rank([middle] + middles, rank, 0)[None]
        both = in_order(all_gather(both, modes, groups), own)
        high, low = hidden(core_left, jnp.swapaxes(both, 0, 1).reshape(carried.shape))

    if count:
        chunks, counts = [prepare(sketch_left)], [1]
        for pair in zip(left_a_arrived, left_b_arrived):
            chunks += [prepare(x, 0) for x in pair]
            counts.append(2)
    else:
        whole = [jnp.concatenate(pair) for pair in zip(left_a_arrived, left_b_arrived)]
        chunks, counts = [prepare(jnp.concatenate([sketch_slices] + whole, axis=1), 0)], [1]
    term = joined(place, high, low, counts, chunks, size * ranks, count)
    result = all_gather_parts(scattered(term), modes, groups)
    if count:
        return settle(place, result, ranks)
    return in_order(jnp.concatenate(result, axis=0), own).reshape(carry_in.shape)


def solution(mesh):
    modes, ranks = mesh.shape["mode"], mesh.shape["rank"]
    in_specs = (P("rank", "mode", None),) * 4 + (P("rank", None),)
    body = functools.partial(shards, modes, ranks)
    return jax.shard_map(body, mesh=mesh, in_specs=in_specs, out_specs=P("rank", None), check_vma=False)
```

```python
import functools

import jax
import jax.numpy as jnp
from jax import lax
from jax.experimental import pallas as pl
from jax.experimental.pallas import tpu as pltpu
from jax.sharding import PartitionSpec as P

F32, BF16 = jnp.float32, jnp.bfloat16
LANES = 128
HBM = pl.BlockSpec(memory_space=pl.ANY)
VMEM = pl.BlockSpec(memory_space=pltpu.VMEM)
SMEM = pl.BlockSpec(memory_space=pltpu.SMEM)


def halves(x):
    high = x.astype(BF16)
    return high, (x - high.astype(F32)).astype(BF16)


def dot(a, b):
    return jnp.dot(a, b, preferred_element_type=F32)


def prepare_kernel(sketch_ref, out_ref, axis=1):
    size = sketch_ref.shape[1 - axis]
    for i in range(sketch_ref.shape[axis]):
        high, low = halves((sketch_ref[:, i, :] if axis else sketch_ref[i]).T)
        out_ref[i, :, :size] = high
        out_ref[i, :, size:] = low


def hidden_loop(core_hbm, spread, high, low, buf, sems, weights):
    rows, slices, _ = core_hbm.shape
    slots, width = buf.shape[0], buf.shape[1] // rows
    steps = slices // width

    def copies(k):
        slot = lax.rem(k, slots)
        return [
            pltpu.make_async_copy(core_hbm.at[:, k * width + u, :], buf.at[slot, pl.ds(u * rows, rows)], sems.at[slot, u])
            for u in range(width)
        ]

    for k in range(min(slots - 1, steps)):
        for copy in copies(k):
            copy.start()
    spread(weights)

    def block(k, _):
        @pl.when(k + slots - 1 < steps)
        def _():
            for copy in copies(k + slots - 1):
                copy.start()

        for copy in copies(k):
            copy.wait()
        h, l = halves(buf[lax.rem(k, slots)])
        h, l = halves(dot(jnp.concatenate([h, h, l], axis=1), weights[...]))
        for u in range(width):
            high[k * width + u] = h[u * rows : (u + 1) * rows]
            low[k * width + u] = l[u * rows : (u + 1) * rows]
        return 0

    lax.fori_loop(0, steps, block, 0)


def spread_whole(carried_ref, weights):
    depth = carried_ref.shape[0]
    h, l = halves(carried_ref[...])
    weights[0:depth] = h
    weights[depth : 2 * depth] = l
    weights[2 * depth :] = h


def first_kernel(core_hbm, carried_ref, sketch_ref, high, low, out, prepared, *scratch):
    hidden_loop(core_hbm, functools.partial(spread_whole, carried_ref), high, low, *scratch)
    prepare_kernel(sketch_ref, prepared)
    out[...] = jnp.zeros_like(out)
    multiply(high, low, [[prepared]], out)


def hidden_kernel(core_hbm, carried_ref, high, low, *scratch):
    hidden_loop(core_hbm, functools.partial(spread_whole, carried_ref), high, low, *scratch)


def spread_pieces(ranks, place_ref, parts, weights):
    own, rank = place_ref[0], place_ref[1]
    _, _, rows, columns = parts[0].shape
    depth, width = weights.shape[0] // 3, columns // ranks
    position = 0
    for part in parts:
        for p in range(part.shape[0]):
            for d in range(ranks):
                source = lax.rem(rank - d + ranks, ranks)
                at = pl.multiple_of(source * (depth // ranks) + (own ^ position) * rows, rows)
                for e in range(ranks):
                    to = pl.ds(pl.multiple_of(lax.rem(source - e + ranks, ranks) * width, width), width)
                    h, l = halves(part[p, d, :, e * width : (e + 1) * width])
                    weights[pl.ds(at, rows), to] = h
                    weights[pl.ds(at + depth, rows), to] = l
                    weights[pl.ds(at + 2 * depth, rows), to] = h
            position += 1


def hidden_of_pieces_kernel(ranks, core_hbm, place_ref, *refs):
    parts, scratch = refs[:-5], refs[-5:]
    hidden_loop(core_hbm, functools.partial(spread_pieces, ranks, place_ref, parts), *scratch)


def multiply(high, low, sketches, out):
    where = [[(ref, i) for ref in refs for i in range(ref.shape[0])] for refs in sketches]
    for start in range(0, high.shape[0], GROUP):
        slices = range(start, min(start + GROUP, high.shape[0]))
        h = jnp.concatenate([high[i] for i in slices], axis=1)
        l = jnp.concatenate([low[i] for i in slices], axis=1)
        sums, highs = [], []
        for places in where:
            both = jnp.concatenate([places[i][0][places[i][1]] for i in slices], axis=0)
            width = both.shape[1] // 2
            result = dot(h, both)
            sums.append(result[:, :width] + result[:, width:])
            highs.append(both[:, :width])
        out[...] += jnp.concatenate(sums, axis=1) + dot(l, jnp.concatenate(highs, axis=1))


def store(place_ref, acc, out):
    if len(out.shape) == 2:
        out[...] = acc[...]
        return
    count, rows, _ = out.shape
    for p in range(count):
        out[p] = acc[pl.ds(pl.multiple_of((place_ref[0] ^ p) * rows, rows), rows), :]


def second_kernel(place_ref, high, low, own_ref, *refs):
    sketches, (out, prepared, acc) = refs[:-3], refs[-3:]
    width = own_ref.shape[1]
    acc[:, :width] = own_ref[...]
    for d, sketch in enumerate(sketches):
        at = slice((d + 1) * width, (d + 2) * width)
        acc[:, at] = jnp.zeros_like(own_ref)
        prepare_kernel(sketch, prepared)
        multiply(high, low, [[prepared]], acc.at[:, at])
    store(place_ref, acc, out)


def joined_kernel(counts, place_ref, high, low, *refs):
    chunks, (out, acc) = list(refs[:-2]), refs[-2:]
    acc[...] = jnp.zeros_like(acc)
    multiply(high, low, [[chunks.pop(0) for _ in range(count)] for count in counts], acc)
    store(place_ref, acc, out)


def settle_kernel(ranks, place_ref, *refs):
    parts, out = refs[:-1], refs[-1]
    _, rows, columns = parts[0].shape
    width = columns // ranks
    position = 0
    for part in parts:
        for p in range(part.shape[0]):
            at = pl.ds(pl.multiple_of((place_ref[0] ^ position) * rows, rows), rows)
            for e in range(ranks):
                to = lax.rem(place_ref[1] - e + ranks, ranks) * width
                out[at, pl.ds(pl.multiple_of(to, width), width)] = part[p, :, e * width : (e + 1) * width]
            position += 1


def hidden_shape(core, columns):
    return (core.shape[1], core.shape[0], columns)


def loop_scratch(core, columns):
    rows, slices, depth = core.shape
    width = 2 - slices % 2
    return [
        pltpu.VMEM((SLOTS, width * rows, depth), F32),
        pltpu.SemaphoreType.DMA((SLOTS, width)),
        pltpu.VMEM((3 * depth, columns), BF16),
    ]


def limit(mib):
    return pltpu.CompilerParams(vmem_limit_bytes=mib << 20)


SLOTS, GROUP = 3, 8


def cost(flops, size):
    return pl.CostEstimate(flops=flops, bytes_accessed=size, transcendentals=0)


def hidden(core, carried, place=None):
    count, slices, depth = core.shape
    columns = (carried if place is None else carried[0]).shape[-1]
    out = jax.ShapeDtypeStruct(hidden_shape(core, columns), BF16)
    if place is None:
        kernel, operands = hidden_kernel, (carried,)
    else:
        ranks = carried[0].shape[1]
        kernel, operands = functools.partial(hidden_of_pieces_kernel, ranks), (place, *carried)
    return pl.pallas_call(
        kernel,
        out_shape=(out, out),
        in_specs=[HBM] + ([VMEM] if place is None else [SMEM] + [VMEM] * len(carried)),
        out_specs=(VMEM, VMEM),
        scratch_shapes=loop_scratch(core, columns),
        compiler_params=limit(32),
        cost_estimate=cost(6 * count * slices * depth * columns, 4 * core.size) if place is None else cost(2 * core.size * columns, 1),
    )(core, *operands)


def product_cost(high, slices, columns):
    return cost(6 * high.shape[1] * slices * high.shape[2] * columns, 4 * high.size)


def first_step(core, carried, sketch):
    size, slices, depth = sketch.shape
    columns = carried.shape[1]
    out = jax.ShapeDtypeStruct(hidden_shape(core, columns), BF16)
    return pl.pallas_call(
        first_kernel,
        out_shape=(out, out, jax.ShapeDtypeStruct((core.shape[0], size), F32)),
        in_specs=[HBM, VMEM, VMEM],
        out_specs=(VMEM,) * 3,
        scratch_shapes=[pltpu.VMEM((slices, depth, 2 * size), BF16)] + loop_scratch(core, columns),
        compiler_params=limit(36),
        cost_estimate=cost(4 * core.size * columns, 1),
    )(core, carried, sketch)


def out_shape(rows, columns, count):
    return jax.ShapeDtypeStruct((count, rows // count, columns) if count else (rows, columns), F32)


def second_product(place, high, low, own, sketches, count):
    size, slices, depth = sketches[0].shape
    rows, columns = high.shape[1], size * (1 + len(sketches))
    return pl.pallas_call(
        second_kernel,
        out_shape=out_shape(rows, columns, count),
        in_specs=[SMEM] + [VMEM] * (3 + len(sketches)),
        out_specs=VMEM,
        scratch_shapes=[pltpu.VMEM((slices, depth, 2 * size), BF16), pltpu.VMEM((rows, columns), F32)],
        compiler_params=limit(24),
        cost_estimate=product_cost(high, slices, columns - size),
    )(place, high, low, own, *sketches)


def joined(place, high, low, counts, chunks, columns, count):
    rows = high.shape[1]
    return pl.pallas_call(
        functools.partial(joined_kernel, counts),
        out_shape=out_shape(rows, columns, count),
        in_specs=[SMEM] + [VMEM] * (2 + len(chunks)),
        out_specs=VMEM,
        scratch_shapes=[pltpu.VMEM((rows, columns), F32)],
        compiler_params=limit(24),
        cost_estimate=product_cost(high, high.shape[0], columns),
    )(place, high, low, *chunks)


def settle(place, parts, ranks):
    _, rows, columns = parts[0].shape
    return pl.pallas_call(
        functools.partial(settle_kernel, ranks),
        out_shape=jax.ShapeDtypeStruct((rows * sum(p.shape[0] for p in parts), columns), F32),
        in_specs=[SMEM] + [VMEM] * len(parts),
        out_specs=VMEM,
        compiler_params=limit(8),
    )(place, *parts)


def prepare(sketch, axis=1):
    slices, size, depth = sketch.shape[axis], sketch.shape[1 - axis], sketch.shape[2]
    return pl.pallas_call(
        functools.partial(prepare_kernel, axis=axis),
        out_shape=jax.ShapeDtypeStruct((slices, depth, 2 * size), BF16),
        in_specs=[VMEM],
        out_specs=VMEM,
        compiler_params=limit(16),
        cost_estimate=cost(0, 8 * sketch.size),
    )(sketch)


def digit_groups(count):
    bits = count.bit_length() - 1
    groups, low = [], 0
    while low < bits:
        width = 1 if low < 2 else min(2, bits - low)
        groups.append((low, width))
        low += width
    return groups


def far_first(digit, width):
    return digit ^ ((digit & 1) << 1) if width == 2 else digit


def piece_of(index, groups):
    piece = 0
    for low, width in groups:
        piece = (piece << width) | far_first((index >> low) & ((1 << width) - 1), width)
    return piece


def partner(x, count, low, width, position):
    distance = far_first(position, width) << low
    return lax.ppermute(x, "mode", [(i, i ^ distance) for i in range(count)])


def shift(x, ranks, d):
    return lax.ppermute(x, "rank", [(i, (i + d) % ranks) for i in range(ranks)])


def reduce_scatter(x, count, groups):
    for low, width in groups:
        size = x.shape[0] >> width
        arrived = [partner(x[d * size : (d + 1) * size], count, low, width, d) for d in range(1, 1 << width)]
        x = sum(arrived, x[:size])
    return x


def all_gather_parts(x, count, groups):
    parts = [x]
    for low, width in reversed(groups):
        x = jnp.concatenate(parts, axis=0)
        parts = [x] + [partner(x, count, low, width, d) for d in range(1, 1 << width)]
    return parts


def all_gather(x, count, groups):
    return jnp.concatenate(all_gather_parts(x, count, groups), axis=0)


def in_order(x, own):
    return jnp.take(x, own ^ jnp.arange(x.shape[0]), axis=0)


def by_rank(blocks, rank, axis):
    joined = jnp.concatenate(blocks[::-1], axis=axis)
    return jnp.roll(joined, (rank + 1) * blocks[0].shape[axis], axis=axis)


def part_groups(modes):
    return [(low, 1) for low in range(min(3, modes.bit_length() - 1))]


def own_part(x, modes, mode):
    groups = part_groups(modes)
    size = x.shape[0] >> len(groups)
    return lax.dynamic_slice_in_dim(x, piece_of(mode, groups) * size, size)


def all_rows(x, parts, modes, rank, mode):
    groups = part_groups(modes)
    own = piece_of(mode, groups)
    blocks = [in_order(all_gather(part[None], modes, groups), own).reshape(x.shape) for part in parts]
    return by_rank([x] + blocks, rank, 0)


def shards(modes, ranks, core_right, sketch_right, core_left, sketch_left, carry_in):
    mode, rank = lax.axis_index("mode"), lax.axis_index("rank")
    groups = digit_groups(modes)
    own = piece_of(mode, groups)
    place = jnp.stack([own, rank])
    slices, size = core_right.shape[1], sketch_right.shape[0]
    early = max(1, slices // 4)
    count = modes if carry_in.shape[0] % (16 * modes) == 0 and size % LANES == 0 else 0

    def shifted(x):
        return [shift(x, ranks, d) for d in range(1, ranks)]

    def scattered(term):
        if not count:
            term = by_rank(jnp.split(term, ranks, axis=1), rank, 1)
            term = in_order(term.reshape((modes, term.shape[0] // modes) + term.shape[1:]), own)
        return reduce_scatter(term, modes, groups)

    sketch_slices = jnp.swapaxes(sketch_left, 0, 1)
    left_a, left_b = sketch_slices[:early], sketch_slices[early:]
    part = own_part(carry_in, modes, mode)
    parts = shifted(part)
    _, right = lax.optimization_barrier((part, sketch_right))
    arrived = shifted(right)
    carried = all_rows(carry_in, parts, modes, rank, mode)
    high, low, term = first_step(core_right, carried, sketch_right)
    arrived, left_a = lax.optimization_barrier((arrived, left_a))
    left_a_arrived = shifted(left_a)
    term = second_product(place, high, low, term, arrived, count)
    middle = scattered(term)
    middle, left_a_arrived, left_b = lax.optimization_barrier((middle, left_a_arrived, left_b))
    middles = shifted(middle)
    left_b_arrived = shifted(left_b)
    if count:
        both = jnp.concatenate([middle] + middles)[None]
        high, low = hidden(core_left, all_gather_parts(both, modes, groups), place)
    else:
        both = by_rank([middle] + middles, rank, 0)[None]
        both = in_order(all_gather(both, modes, groups), own)
        high, low = hidden(core_left, jnp.swapaxes(both, 0, 1).reshape(carried.shape))

    if count:
        chunks, counts = [prepare(sketch_left)], [1]
        for pair in zip(left_a_arrived, left_b_arrived):
            chunks += [prepare(x, 0) for x in pair]
            counts.append(2)
    else:
        whole = [jnp.concatenate(pair) for pair in zip(left_a_arrived, left_b_arrived)]
        chunks, counts = [prepare(jnp.concatenate([sketch_slices] + whole, axis=1), 0)], [1]
    term = joined(place, high, low, counts, chunks, size * ranks, count)
    result = all_gather_parts(scattered(term), modes, groups)
    if count:
        return settle(place, result, ranks)
    return in_order(jnp.concatenate(result, axis=0), own).reshape(carry_in.shape)


def solution(mesh):
    modes, ranks = mesh.shape["mode"], mesh.shape["rank"]
    in_specs = (P("rank", "mode", None),) * 4 + (P("rank", None),)
    body = functools.partial(shards, modes, ranks)
    return jax.shard_map(body, mesh=mesh, in_specs=in_specs, out_specs=P("rank", None), check_vma=False)
```

```python
import functools

import jax
import jax.numpy as jnp
from jax import lax
from jax.experimental import pallas as pl
from jax.experimental.pallas import tpu as pltpu
from jax.sharding import PartitionSpec as P

F32, BF16 = jnp.float32, jnp.bfloat16
LANES = 128
HBM = pl.BlockSpec(memory_space=pl.ANY)
VMEM = pl.BlockSpec(memory_space=pltpu.VMEM)
SMEM = pl.BlockSpec(memory_space=pltpu.SMEM)


def halves(x):
    high = x.astype(BF16)
    return high, (x - high.astype(F32)).astype(BF16)


def dot(a, b):
    return jnp.dot(a, b, preferred_element_type=F32)


def prepare_kernel(sketch_ref, out_ref, axis=1):
    size = sketch_ref.shape[1 - axis]
    for i in range(sketch_ref.shape[axis]):
        high, low = halves((sketch_ref[:, i, :] if axis else sketch_ref[i]).T)
        out_ref[i, :, :size] = high
        out_ref[i, :, size:] = low


def hidden_loop(core_hbm, spread, high, low, buf, sems, weights):
    rows, slices, _ = core_hbm.shape
    slots, width = buf.shape[0], buf.shape[1] // rows
    steps = slices // width

    def copies(k):
        slot = lax.rem(k, slots)
        return [
            pltpu.make_async_copy(core_hbm.at[:, k * width + u, :], buf.at[slot, pl.ds(u * rows, rows)], sems.at[slot, u])
            for u in range(width)
        ]

    for k in range(min(slots - 1, steps)):
        for copy in copies(k):
            copy.start()
    spread(weights)

    def block(k, _):
        @pl.when(k + slots - 1 < steps)
        def _():
            for copy in copies(k + slots - 1):
                copy.start()

        for copy in copies(k):
            copy.wait()
        h, l = halves(buf[lax.rem(k, slots)])
        both = dot(h, weights[...])
        columns = both.shape[1] // 2
        h, l = halves(both[:, :columns] + both[:, columns:] + dot(l, weights[:, :columns]))
        for u in range(width):
            high[k * width + u] = h[u * rows : (u + 1) * rows]
            low[k * width + u] = l[u * rows : (u + 1) * rows]
        return 0

    lax.fori_loop(0, steps, block, 0)


def spread_whole(carried_ref, weights):
    columns = carried_ref.shape[1]
    weights[:, :columns], weights[:, columns:] = halves(carried_ref[...])


def first_kernel(core_hbm, carried_ref, sketch_ref, high, low, out, prepared, *scratch):
    hidden_loop(core_hbm, functools.partial(spread_whole, carried_ref), high, low, *scratch)
    prepare_kernel(sketch_ref, prepared)
    out[...] = jnp.zeros_like(out)
    multiply(high, low, [[prepared]], out)


def hidden_kernel(core_hbm, carried_ref, high, low, *scratch):
    hidden_loop(core_hbm, functools.partial(spread_whole, carried_ref), high, low, *scratch)


def spread_pieces(ranks, place_ref, parts, weights):
    own, rank = place_ref[0], place_ref[1]
    _, _, rows, columns = parts[0].shape
    depth, width = weights.shape[0], columns // ranks
    position = 0
    for part in parts:
        for p in range(part.shape[0]):
            for d in range(ranks):
                source = lax.rem(rank - d + ranks, ranks)
                at = pl.multiple_of(source * (depth // ranks) + (own ^ position) * rows, rows)
                for e in range(ranks):
                    to = pl.multiple_of(lax.rem(source - e + ranks, ranks) * width, width)
                    h, l = halves(part[p, d, :, e * width : (e + 1) * width])
                    weights[pl.ds(at, rows), pl.ds(to, width)] = h
                    weights[pl.ds(at, rows), pl.ds(to + columns, width)] = l
            position += 1


def hidden_of_pieces_kernel(ranks, core_hbm, place_ref, *refs):
    parts, scratch = refs[:-5], refs[-5:]
    hidden_loop(core_hbm, functools.partial(spread_pieces, ranks, place_ref, parts), *scratch)


def multiply(high, low, sketches, out):
    where = [[(ref, i) for ref in refs for i in range(ref.shape[0])] for refs in sketches]
    for start in range(0, high.shape[0], GROUP):
        slices = range(start, min(start + GROUP, high.shape[0]))
        h = jnp.concatenate([high[i] for i in slices], axis=1)
        l = jnp.concatenate([low[i] for i in slices], axis=1)
        sums, highs = [], []
        for places in where:
            both = jnp.concatenate([places[i][0][places[i][1]] for i in slices], axis=0)
            width = both.shape[1] // 2
            result = dot(h, both)
            sums.append(result[:, :width] + result[:, width:])
            highs.append(both[:, :width])
        out[...] += jnp.concatenate(sums, axis=1) + dot(l, jnp.concatenate(highs, axis=1))


def store(place_ref, acc, out):
    if len(out.shape) == 2:
        out[...] = acc[...]
        return
    count, rows, _ = out.shape
    for p in range(count):
        out[p] = acc[pl.ds(pl.multiple_of((place_ref[0] ^ p) * rows, rows), rows), :]


def second_kernel(place_ref, high, low, own_ref, *refs):
    sketches, (out, prepared, acc) = refs[:-3], refs[-3:]
    width = own_ref.shape[1]
    acc[:, :width] = own_ref[...]
    for d, sketch in enumerate(sketches):
        at = slice((d + 1) * width, (d + 2) * width)
        acc[:, at] = jnp.zeros_like(own_ref)
        prepare_kernel(sketch, prepared)
        multiply(high, low, [[prepared]], acc.at[:, at])
    store(place_ref, acc, out)


def joined_kernel(counts, place_ref, high, low, *refs):
    chunks, (out, acc) = list(refs[:-2]), refs[-2:]
    acc[...] = jnp.zeros_like(acc)
    multiply(high, low, [[chunks.pop(0) for _ in range(count)] for count in counts], acc)
    store(place_ref, acc, out)


def settle_kernel(ranks, place_ref, *refs):
    parts, out = refs[:-1], refs[-1]
    _, rows, columns = parts[0].shape
    width = columns // ranks
    position = 0
    for part in parts:
        for p in range(part.shape[0]):
            at = pl.ds(pl.multiple_of((place_ref[0] ^ position) * rows, rows), rows)
            for e in range(ranks):
                to = lax.rem(place_ref[1] - e + ranks, ranks) * width
                out[at, pl.ds(pl.multiple_of(to, width), width)] = part[p, :, e * width : (e + 1) * width]
            position += 1


def hidden_shape(core, columns):
    return (core.shape[1], core.shape[0], columns)


def loop_scratch(core, columns):
    rows, slices, depth = core.shape
    width = 2 - slices % 2
    return [
        pltpu.VMEM((SLOTS, width * rows, depth), F32),
        pltpu.SemaphoreType.DMA((SLOTS, width)),
        pltpu.VMEM((depth, 2 * columns), BF16),
    ]


def limit(mib):
    return pltpu.CompilerParams(vmem_limit_bytes=mib << 20)


SLOTS, GROUP = 3, 8


def cost(flops, size):
    return pl.CostEstimate(flops=flops, bytes_accessed=size, transcendentals=0)


def hidden(core, carried, place=None):
    count, slices, depth = core.shape
    columns = (carried if place is None else carried[0]).shape[-1]
    out = jax.ShapeDtypeStruct(hidden_shape(core, columns), BF16)
    if place is None:
        kernel, operands = hidden_kernel, (carried,)
    else:
        ranks = carried[0].shape[1]
        kernel, operands = functools.partial(hidden_of_pieces_kernel, ranks), (place, *carried)
    return pl.pallas_call(
        kernel,
        out_shape=(out, out),
        in_specs=[HBM] + ([VMEM] if place is None else [SMEM] + [VMEM] * len(carried)),
        out_specs=(VMEM, VMEM),
        scratch_shapes=loop_scratch(core, columns),
        compiler_params=limit(32),
        cost_estimate=cost(6 * count * slices * depth * columns, 4 * core.size) if place is None else cost(2 * core.size * columns, 1),
    )(core, *operands)


def product_cost(high, slices, columns):
    return cost(6 * high.shape[1] * slices * high.shape[2] * columns, 4 * high.size)


def first_step(core, carried, sketch):
    size, slices, depth = sketch.shape
    columns = carried.shape[1]
    out = jax.ShapeDtypeStruct(hidden_shape(core, columns), BF16)
    return pl.pallas_call(
        first_kernel,
        out_shape=(out, out, jax.ShapeDtypeStruct((core.shape[0], size), F32)),
        in_specs=[HBM, VMEM, VMEM],
        out_specs=(VMEM,) * 3,
        scratch_shapes=[pltpu.VMEM((slices, depth, 2 * size), BF16)] + loop_scratch(core, columns),
        compiler_params=limit(36),
        cost_estimate=cost(28 * core.size * columns // 8, 1),
    )(core, carried, sketch)


def out_shape(rows, columns, count):
    return jax.ShapeDtypeStruct((count, rows // count, columns) if count else (rows, columns), F32)


def second_product(place, high, low, own, sketches, count):
    size, slices, depth = sketches[0].shape
    rows, columns = high.shape[1], size * (1 + len(sketches))
    return pl.pallas_call(
        second_kernel,
        out_shape=out_shape(rows, columns, count),
        in_specs=[SMEM] + [VMEM] * (3 + len(sketches)),
        out_specs=VMEM,
        scratch_shapes=[pltpu.VMEM((slices, depth, 2 * size), BF16), pltpu.VMEM((rows, columns), F32)],
        compiler_params=limit(24),
        cost_estimate=product_cost(high, slices, columns - size),
    )(place, high, low, own, *sketches)


def joined(place, high, low, counts, chunks, columns, count):
    rows = high.shape[1]
    return pl.pallas_call(
        functools.partial(joined_kernel, counts),
        out_shape=out_shape(rows, columns, count),
        in_specs=[SMEM] + [VMEM] * (2 + len(chunks)),
        out_specs=VMEM,
        scratch_shapes=[pltpu.VMEM((rows, columns), F32)],
        compiler_params=limit(24),
        cost_estimate=product_cost(high, high.shape[0], columns),
    )(place, high, low, *chunks)


def settle(place, parts, ranks):
    _, rows, columns = parts[0].shape
    return pl.pallas_call(
        functools.partial(settle_kernel, ranks),
        out_shape=jax.ShapeDtypeStruct((rows * sum(p.shape[0] for p in parts), columns), F32),
        in_specs=[SMEM] + [VMEM] * len(parts),
        out_specs=VMEM,
        compiler_params=limit(8),
    )(place, *parts)


def prepare(sketch, axis=1):
    slices, size, depth = sketch.shape[axis], sketch.shape[1 - axis], sketch.shape[2]
    return pl.pallas_call(
        functools.partial(prepare_kernel, axis=axis),
        out_shape=jax.ShapeDtypeStruct((slices, depth, 2 * size), BF16),
        in_specs=[VMEM],
        out_specs=VMEM,
        compiler_params=limit(16),
        cost_estimate=cost(0, 8 * sketch.size),
    )(sketch)


def digit_groups(count):
    bits = count.bit_length() - 1
    groups, low = [], 0
    while low < bits:
        width = 1 if low < 2 else min(2, bits - low)
        groups.append((low, width))
        low += width
    return groups


def far_first(digit, width):
    return digit ^ ((digit & 1) << 1) if width == 2 else digit


def piece_of(index, groups):
    piece = 0
    for low, width in groups:
        piece = (piece << width) | far_first((index >> low) & ((1 << width) - 1), width)
    return piece


def partner(x, count, low, width, position):
    distance = far_first(position, width) << low
    return lax.ppermute(x, "mode", [(i, i ^ distance) for i in range(count)])


def shift(x, ranks, d):
    return lax.ppermute(x, "rank", [(i, (i + d) % ranks) for i in range(ranks)])


def reduce_scatter(x, count, groups):
    for low, width in groups:
        size = x.shape[0] >> width
        arrived = [partner(x[d * size : (d + 1) * size], count, low, width, d) for d in range(1, 1 << width)]
        x = sum(arrived, x[:size])
    return x


def all_gather_parts(x, count, groups):
    parts = [x]
    for low, width in reversed(groups):
        x = jnp.concatenate(parts, axis=0)
        parts = [x] + [partner(x, count, low, width, d) for d in range(1, 1 << width)]
    return parts


def all_gather(x, count, groups):
    return jnp.concatenate(all_gather_parts(x, count, groups), axis=0)


def in_order(x, own):
    return jnp.take(x, own ^ jnp.arange(x.shape[0]), axis=0)


def by_rank(blocks, rank, axis):
    joined = jnp.concatenate(blocks[::-1], axis=axis)
    return jnp.roll(joined, (rank + 1) * blocks[0].shape[axis], axis=axis)


def part_groups(modes):
    return [(low, 1) for low in range(min(4, modes.bit_length() - 1))]


def own_part(x, modes, mode):
    groups = part_groups(modes)
    size = x.shape[0] >> len(groups)
    return lax.dynamic_slice_in_dim(x, piece_of(mode, groups) * size, size)


def all_rows(x, parts, modes, rank, mode):
    groups = part_groups(modes)
    own = piece_of(mode, groups)
    blocks = [in_order(all_gather(part[None], modes, groups), own).reshape(x.shape) for part in parts]
    return by_rank([x] + blocks, rank, 0)


def shards(modes, ranks, core_right, sketch_right, core_left, sketch_left, carry_in):
    mode, rank = lax.axis_index("mode"), lax.axis_index("rank")
    groups = digit_groups(modes)
    own = piece_of(mode, groups)
    place = jnp.stack([own, rank])
    slices, size = core_right.shape[1], sketch_right.shape[0]
    early = max(1, slices // 4)
    count = modes if carry_in.shape[0] % (16 * modes) == 0 and size % LANES == 0 else 0

    def shifted(x):
        return [shift(x, ranks, d) for d in range(1, ranks)]

    def scattered(term):
        if not count:
            term = by_rank(jnp.split(term, ranks, axis=1), rank, 1)
            term = in_order(term.reshape((modes, term.shape[0] // modes) + term.shape[1:]), own)
        return reduce_scatter(term, modes, groups)

    sketch_slices = jnp.swapaxes(sketch_left, 0, 1)
    left_a, left_b = sketch_slices[:early], sketch_slices[early:]
    part = own_part(carry_in, modes, mode)
    parts = shifted(part)
    _, right = lax.optimization_barrier((part, sketch_right))
    arrived = shifted(right)
    carried = all_rows(carry_in, parts, modes, rank, mode)
    high, low, term = first_step(core_right, carried, sketch_right)
    arrived, left_a = lax.optimization_barrier((arrived, left_a))
    left_a_arrived = shifted(left_a)
    term = second_product(place, high, low, term, arrived, count)
    middle = scattered(term)
    middle, left_a_arrived, left_b = lax.optimization_barrier((middle, left_a_arrived, left_b))
    middles = shifted(middle)
    left_b_arrived = shifted(left_b)
    if count:
        both = jnp.concatenate([middle] + middles)[None]
        high, low = hidden(core_left, all_gather_parts(both, modes, groups), place)
    else:
        both = by_rank([middle] + middles, rank, 0)[None]
        both = in_order(all_gather(both, modes, groups), own)
        high, low = hidden(core_left, jnp.swapaxes(both, 0, 1).reshape(carried.shape))

    if count:
        chunks, counts = [prepare(sketch_left)], [1]
        for pair in zip(left_a_arrived, left_b_arrived):
            chunks += [prepare(x, 0) for x in pair]
            counts.append(2)
    else:
        whole = [jnp.concatenate(pair) for pair in zip(left_a_arrived, left_b_arrived)]
        chunks, counts = [prepare(jnp.concatenate([sketch_slices] + whole, axis=1), 0)], [1]
    term = joined(place, high, low, counts, chunks, size * ranks, count)
    result = all_gather_parts(scattered(term), modes, groups)
    if count:
        return settle(place, result, ranks)
    return in_order(jnp.concatenate(result, axis=0), own).reshape(carry_in.shape)


def solution(mesh):
    modes, ranks = mesh.shape["mode"], mesh.shape["rank"]
    in_specs = (P("rank", "mode", None),) * 4 + (P("rank", None),)
    body = functools.partial(shards, modes, ranks)
    return jax.shard_map(body, mesh=mesh, in_specs=in_specs, out_specs=P("rank", None), check_vma=False)
```

```python
import functools

import jax
import jax.numpy as jnp
from jax import lax
from jax.experimental import pallas as pl
from jax.experimental.pallas import tpu as pltpu
from jax.sharding import PartitionSpec as P

F32, BF16 = jnp.float32, jnp.bfloat16
LANES = 128
HBM = pl.BlockSpec(memory_space=pl.ANY)
VMEM = pl.BlockSpec(memory_space=pltpu.VMEM)
SMEM = pl.BlockSpec(memory_space=pltpu.SMEM)


def halves(x):
    high = x.astype(BF16)
    return high, (x - high.astype(F32)).astype(BF16)


def dot(a, b):
    return jnp.dot(a, b, preferred_element_type=F32)


def prepare_kernel(sketch_ref, out_ref, axis=1):
    size = sketch_ref.shape[1 - axis]
    for i in range(sketch_ref.shape[axis]):
        high, low = halves((sketch_ref[:, i, :] if axis else sketch_ref[i]).T)
        out_ref[i, :, :size] = high
        out_ref[i, :, size:] = low


def hidden_loop(core_hbm, spread, high, low, buf, sems, weights):
    rows, slices, _ = core_hbm.shape
    slots, width = buf.shape[0], buf.shape[1] // rows
    steps = slices // width

    def copies(k):
        slot = lax.rem(k, slots)
        return [
            pltpu.make_async_copy(core_hbm.at[:, k * width + u, :], buf.at[slot, pl.ds(u * rows, rows)], sems.at[slot, u])
            for u in range(width)
        ]

    for k in range(min(slots - 1, steps)):
        for copy in copies(k):
            copy.start()
    spread(weights)

    def block(k, _):
        @pl.when(k + slots - 1 < steps)
        def _():
            for copy in copies(k + slots - 1):
                copy.start()

        for copy in copies(k):
            copy.wait()
        h, l = halves(buf[lax.rem(k, slots)])
        both = dot(h, weights[...])
        columns = both.shape[1] // 2
        h, l = halves(both[:, :columns] + both[:, columns:] + dot(l, weights[:, :columns]))
        for u in range(width):
            high[k * width + u] = h[u * rows : (u + 1) * rows]
            low[k * width + u] = l[u * rows : (u + 1) * rows]
        return 0

    lax.fori_loop(0, steps, block, 0)


def spread_whole(carried_ref, weights):
    columns = carried_ref.shape[1]
    weights[:, :columns], weights[:, columns:] = halves(carried_ref[...])


def first_kernel(core_hbm, carried_ref, sketch_ref, high, low, out, prepared, *scratch):
    hidden_loop(core_hbm, functools.partial(spread_whole, carried_ref), high, low, *scratch)
    prepare_kernel(sketch_ref, prepared)
    out[...] = jnp.zeros_like(out)
    multiply(high, low, [[prepared]], out)


def hidden_kernel(core_hbm, carried_ref, high, low, *scratch):
    hidden_loop(core_hbm, functools.partial(spread_whole, carried_ref), high, low, *scratch)


def spread_pieces(ranks, place_ref, parts, weights):
    own, rank = place_ref[0], place_ref[1]
    _, _, rows, columns = parts[0].shape
    depth, width = weights.shape[0], columns // ranks
    position = 0
    for part in parts:
        for p in range(part.shape[0]):
            for d in range(ranks):
                source = lax.rem(rank - d + ranks, ranks)
                at = pl.multiple_of(source * (depth // ranks) + (own ^ position) * rows, rows)
                for e in range(ranks):
                    to = pl.multiple_of(lax.rem(source - e + ranks, ranks) * width, width)
                    h, l = halves(part[p, d, :, e * width : (e + 1) * width])
                    weights[pl.ds(at, rows), pl.ds(to, width)] = h
                    weights[pl.ds(at, rows), pl.ds(to + columns, width)] = l
            position += 1


def hidden_of_pieces_kernel(ranks, core_hbm, place_ref, *refs):
    parts, scratch = refs[:-5], refs[-5:]
    hidden_loop(core_hbm, functools.partial(spread_pieces, ranks, place_ref, parts), *scratch)


def multiply(high, low, sketches, out):
    where = [[(ref, i) for ref in refs for i in range(ref.shape[0])] for refs in sketches]
    for start in range(0, high.shape[0], GROUP):
        slices = range(start, min(start + GROUP, high.shape[0]))
        h = jnp.concatenate([high[i] for i in slices], axis=1)
        l = jnp.concatenate([low[i] for i in slices], axis=1)
        sums, highs = [], []
        for places in where:
            both = jnp.concatenate([places[i][0][places[i][1]] for i in slices], axis=0)
            width = both.shape[1] // 2
            result = dot(h, both)
            sums.append(result[:, :width] + result[:, width:])
            highs.append(both[:, :width])
        out[...] += jnp.concatenate(sums, axis=1) + dot(l, jnp.concatenate(highs, axis=1))


def store(place_ref, acc, out):
    if len(out.shape) == 2:
        out[...] = acc[...]
        return
    count, rows, _ = out.shape
    for p in range(count):
        out[p] = acc[pl.ds(pl.multiple_of((place_ref[0] ^ p) * rows, rows), rows), :]


def second_kernel(place_ref, high, low, own_ref, *refs):
    sketches, (out, prepared, acc) = refs[:-3], refs[-3:]
    width = own_ref.shape[1]
    acc[:, :width] = own_ref[...]
    for d, sketch in enumerate(sketches):
        at = slice((d + 1) * width, (d + 2) * width)
        acc[:, at] = jnp.zeros_like(own_ref)
        prepare_kernel(sketch, prepared)
        multiply(high, low, [[prepared]], acc.at[:, at])
    store(place_ref, acc, out)


def joined_kernel(counts, place_ref, high, low, *refs):
    chunks, (out, acc) = list(refs[:-2]), refs[-2:]
    acc[...] = jnp.zeros_like(acc)
    multiply(high, low, [[chunks.pop(0) for _ in range(count)] for count in counts], acc)
    store(place_ref, acc, out)


def settle_kernel(ranks, place_ref, *refs):
    parts, out = refs[:-1], refs[-1]
    _, rows, columns = parts[0].shape
    width = columns // ranks
    position = 0
    for part in parts:
        for p in range(part.shape[0]):
            at = pl.ds(pl.multiple_of((place_ref[0] ^ position) * rows, rows), rows)
            for e in range(ranks):
                to = lax.rem(place_ref[1] - e + ranks, ranks) * width
                out[at, pl.ds(pl.multiple_of(to, width), width)] = part[p, :, e * width : (e + 1) * width]
            position += 1


def hidden_shape(core, columns):
    return (core.shape[1], core.shape[0], columns)


def loop_scratch(core, columns):
    rows, slices, depth = core.shape
    width = 2 - slices % 2
    return [
        pltpu.VMEM((SLOTS, width * rows, depth), F32),
        pltpu.SemaphoreType.DMA((SLOTS, width)),
        pltpu.VMEM((depth, 2 * columns), BF16),
    ]


def limit(mib):
    return pltpu.CompilerParams(vmem_limit_bytes=mib << 20)


SLOTS, GROUP = 4, 8


def cost(flops, size):
    return pl.CostEstimate(flops=flops, bytes_accessed=size, transcendentals=0)


def hidden(core, carried, place=None):
    count, slices, depth = core.shape
    columns = (carried if place is None else carried[0]).shape[-1]
    out = jax.ShapeDtypeStruct(hidden_shape(core, columns), BF16)
    if place is None:
        kernel, operands = hidden_kernel, (carried,)
    else:
        ranks = carried[0].shape[1]
        kernel, operands = functools.partial(hidden_of_pieces_kernel, ranks), (place, *carried)
    return pl.pallas_call(
        kernel,
        out_shape=(out, out),
        in_specs=[HBM] + ([VMEM] if place is None else [SMEM] + [VMEM] * len(carried)),
        out_specs=(VMEM, VMEM),
        scratch_shapes=loop_scratch(core, columns),
        compiler_params=limit(40),
        cost_estimate=cost(6 * count * slices * depth * columns, 4 * core.size) if place is None else cost(2 * core.size * columns, 1),
    )(core, *operands)


def product_cost(high, slices, columns):
    return cost(6 * high.shape[1] * slices * high.shape[2] * columns, 4 * high.size)


def first_step(core, carried, sketch):
    size, slices, depth = sketch.shape
    columns = carried.shape[1]
    out = jax.ShapeDtypeStruct(hidden_shape(core, columns), BF16)
    return pl.pallas_call(
        first_kernel,
        out_shape=(out, out, jax.ShapeDtypeStruct((core.shape[0], size), F32)),
        in_specs=[HBM, VMEM, VMEM],
        out_specs=(VMEM,) * 3,
        scratch_shapes=[pltpu.VMEM((slices, depth, 2 * size), BF16)] + loop_scratch(core, columns),
        compiler_params=limit(40),
        cost_estimate=cost(28 * core.size * columns // 8, 1),
    )(core, carried, sketch)


def out_shape(rows, columns, count):
    return jax.ShapeDtypeStruct((count, rows // count, columns) if count else (rows, columns), F32)


def second_product(place, high, low, own, sketches, count):
    size, slices, depth = sketches[0].shape
    rows, columns = high.shape[1], size * (1 + len(sketches))
    return pl.pallas_call(
        second_kernel,
        out_shape=out_shape(rows, columns, count),
        in_specs=[SMEM] + [VMEM] * (3 + len(sketches)),
        out_specs=VMEM,
        scratch_shapes=[pltpu.VMEM((slices, depth, 2 * size), BF16), pltpu.VMEM((rows, columns), F32)],
        compiler_params=limit(24),
        cost_estimate=product_cost(high, slices, columns - size),
    )(place, high, low, own, *sketches)


def joined(place, high, low, counts, chunks, columns, count):
    rows = high.shape[1]
    return pl.pallas_call(
        functools.partial(joined_kernel, counts),
        out_shape=out_shape(rows, columns, count),
        in_specs=[SMEM] + [VMEM] * (2 + len(chunks)),
        out_specs=VMEM,
        scratch_shapes=[pltpu.VMEM((rows, columns), F32)],
        compiler_params=limit(24),
        cost_estimate=product_cost(high, high.shape[0], columns),
    )(place, high, low, *chunks)


def settle(place, parts, ranks):
    _, rows, columns = parts[0].shape
    return pl.pallas_call(
        functools.partial(settle_kernel, ranks),
        out_shape=jax.ShapeDtypeStruct((rows * sum(p.shape[0] for p in parts), columns), F32),
        in_specs=[SMEM] + [VMEM] * len(parts),
        out_specs=VMEM,
        compiler_params=limit(8),
    )(place, *parts)


def prepare(sketch, axis=1):
    slices, size, depth = sketch.shape[axis], sketch.shape[1 - axis], sketch.shape[2]
    return pl.pallas_call(
        functools.partial(prepare_kernel, axis=axis),
        out_shape=jax.ShapeDtypeStruct((slices, depth, 2 * size), BF16),
        in_specs=[VMEM],
        out_specs=VMEM,
        compiler_params=limit(16),
        cost_estimate=cost(0, 8 * sketch.size),
    )(sketch)


def digit_groups(count):
    bits = count.bit_length() - 1
    groups, low = [], 0
    while low < bits:
        width = 1 if low < 2 else min(2, bits - low)
        groups.append((low, width))
        low += width
    return groups


def far_first(digit, width):
    return digit ^ ((digit & 1) << 1) if width == 2 else digit


def piece_of(index, groups):
    piece = 0
    for low, width in groups:
        piece = (piece << width) | far_first((index >> low) & ((1 << width) - 1), width)
    return piece


def partner(x, count, low, width, position):
    distance = far_first(position, width) << low
    return lax.ppermute(x, "mode", [(i, i ^ distance) for i in range(count)])


def shift(x, ranks, d):
    return lax.ppermute(x, "rank", [(i, (i + d) % ranks) for i in range(ranks)])


def reduce_scatter(x, count, groups):
    for low, width in groups:
        size = x.shape[0] >> width
        arrived = [partner(x[d * size : (d + 1) * size], count, low, width, d) for d in range(1, 1 << width)]
        x = sum(arrived, x[:size])
    return x


def all_gather_parts(x, count, groups):
    parts = [x]
    for low, width in reversed(groups):
        x = jnp.concatenate(parts, axis=0)
        parts = [x] + [partner(x, count, low, width, d) for d in range(1, 1 << width)]
    return parts


def all_gather(x, count, groups):
    return jnp.concatenate(all_gather_parts(x, count, groups), axis=0)


def in_order(x, own):
    return jnp.take(x, own ^ jnp.arange(x.shape[0]), axis=0)


def by_rank(blocks, rank, axis):
    joined = jnp.concatenate(blocks[::-1], axis=axis)
    return jnp.roll(joined, (rank + 1) * blocks[0].shape[axis], axis=axis)


def part_groups(modes):
    return [(low, 1) for low in range(min(4, modes.bit_length() - 1))]


def own_part(x, modes, mode):
    groups = part_groups(modes)
    size = x.shape[0] >> len(groups)
    return lax.dynamic_slice_in_dim(x, piece_of(mode, groups) * size, size)


def all_rows(x, parts, modes, rank, mode):
    groups = part_groups(modes)
    own = piece_of(mode, groups)
    blocks = [in_order(all_gather(part[None], modes, groups), own).reshape(x.shape) for part in parts]
    return by_rank([x] + blocks, rank, 0)


def shards(modes, ranks, core_right, sketch_right, core_left, sketch_left, carry_in):
    mode, rank = lax.axis_index("mode"), lax.axis_index("rank")
    groups = digit_groups(modes)
    own = piece_of(mode, groups)
    place = jnp.stack([own, rank])
    slices, size = core_right.shape[1], sketch_right.shape[0]
    early = max(1, slices // 4)
    count = modes if carry_in.shape[0] % (16 * modes) == 0 and size % LANES == 0 else 0

    def shifted(x):
        return [shift(x, ranks, d) for d in range(1, ranks)]

    def scattered(term):
        if not count:
            term = by_rank(jnp.split(term, ranks, axis=1), rank, 1)
            term = in_order(term.reshape((modes, term.shape[0] // modes) + term.shape[1:]), own)
        return reduce_scatter(term, modes, groups)

    sketch_slices = jnp.swapaxes(sketch_left, 0, 1)
    left_a, left_b = sketch_slices[:early], sketch_slices[early:]
    part = own_part(carry_in, modes, mode)
    parts = shifted(part)
    _, right = lax.optimization_barrier((part, sketch_right))
    arrived = shifted(right)
    carried = all_rows(carry_in, parts, modes, rank, mode)
    high, low, term = first_step(core_right, carried, sketch_right)
    arrived, left_a = lax.optimization_barrier((arrived, left_a))
    left_a_arrived = shifted(left_a)
    term = second_product(place, high, low, term, arrived, count)
    middle = scattered(term)
    middle, left_a_arrived, left_b = lax.optimization_barrier((middle, left_a_arrived, left_b))
    middles = shifted(middle)
    left_b_arrived = shifted(left_b)
    if count:
        both = jnp.concatenate([middle] + middles)[None]
        high, low = hidden(core_left, all_gather_parts(both, modes, groups), place)
    else:
        both = by_rank([middle] + middles, rank, 0)[None]
        both = in_order(all_gather(both, modes, groups), own)
        high, low = hidden(core_left, jnp.swapaxes(both, 0, 1).reshape(carried.shape))

    if count:
        chunks, counts = [prepare(sketch_left)], [1]
        for pair in zip(left_a_arrived, left_b_arrived):
            chunks += [prepare(x, 0) for x in pair]
            counts.append(2)
    else:
        whole = [jnp.concatenate(pair) for pair in zip(left_a_arrived, left_b_arrived)]
        chunks, counts = [prepare(jnp.concatenate([sketch_slices] + whole, axis=1), 0)], [1]
    term = joined(place, high, low, counts, chunks, size * ranks, count)
    result = all_gather_parts(scattered(term), modes, groups)
    if count:
        return settle(place, result, ranks)
    return in_order(jnp.concatenate(result, axis=0), own).reshape(carry_in.shape)


def solution(mesh):
    modes, ranks = mesh.shape["mode"], mesh.shape["rank"]
    in_specs = (P("rank", "mode", None),) * 4 + (P("rank", None),)
    body = functools.partial(shards, modes, ranks)
    return jax.shard_map(body, mesh=mesh, in_specs=in_specs, out_specs=P("rank", None), check_vma=False)
```
